32 devices in a mesh: basin: 2 (over y), row: 4 (over z), col: 2 (over x), sub: 2 (over core).
Axes of the slice: x: 2, y: 2, z: 4, core: 2. Of those that a mesh axis runs over, the one named last changes fastest.
Arguments:
- water_depth: float32 [256, 128, 128], P(('basin', 'row', 'col', 'sub')), parts along dimension 0, may hold values from 0.1 to 3
- flow_east: float32 [256, 128, 128], P(('basin', 'row', 'col', 'sub')), parts along dimension 0, may hold values from -3 to 3
- flow_south: float32 [256, 128, 128], P(('basin', 'row', 'col', 'sub')), parts along dimension 0, may hold values from -3 to 3
- bed_level: float32 [256, 128, 128], P(('basin', 'row', 'col', 'sub')), parts along dimension 0, may hold values from -2 to 2
- manning_n: float32 [256, 128, 128], P(('basin', 'row', 'col', 'sub')), parts along dimension 0, may hold values from 0.03 to 0.15
- placed_before: int32 [256], P('basin'), parts along dimension 0, may hold values from 0 to 127, as said below
- placed_after: int32 [256], P('basin'), parts along dimension 0, may hold values from 0 to 127, as said below
- wet_tiles: int32 [256], P('basin'), parts along dimension 0, may hold values 0 or 1
Outputs:
- new_depth: float32 [256, 128, 128], P(('basin', 'row', 'col', 'sub')), parts along dimension 0
- new_flow_east: float32 [256, 128, 128], P(('basin', 'row', 'col', 'sub')), parts along dimension 0
- new_flow_south: float32 [256, 128, 128], P(('basin', 'row', 'col', 'sub')), parts along dimension 0
The draws below stay inside these ranges and needn't reach their ends.
There are 2 independent parts, one for each index of `basin`. The reference program is written for one: setup_inputs(seed, part) draws one part's arguments, and reference() takes and returns one part's arrays. A program takes and returns all parts, laid end to end along the dimension named above; each array names one. Nothing has to cross between parts.
Inputs may be any that keep to these rules, and one draw needn't show every extreme that they name: placed_before holds every tile once. Slot s lies on the device of index s // 8 over row, col and sub together; the tiles of tile row r sit on the devices of row index r. placed_after holds every tile once. A tile either keeps its slot of placed_before or goes to a slot on another device of the same row index. Each device gives up exactly 4 tiles and takes exactly 4, at most 2 of them from any one device.
All inputs are finite; a program needn't handle non-finite values.
Results may differ from the reference program's by a relative error of at most 0.00002.
Values sent between devices are 32-bit elements; how exact they have to be, the bound alone decides.
A program may use at most 64 MiB of HBM per device.

```python
import math
import jax
import jax.numpy as jnp

TS = 128
TILE_DEV = 8
STEPS = 6
LANES = 4
GR = 4
GC = 32
TILES = 128
MOVE_OUT = 4


def tile_layouts(key):
    base_key = jax.random.fold_in(key, 11)
    key_rows, key_labels, key_offsets, key_leave = jax.random.split(base_key, 4)
    row_ids = jnp.arange(GR, dtype=jnp.int32)
    orders = jax.vmap(lambda sub_key: jax.random.permutation(sub_key, GC))(jax.random.split(key_rows, GR)).astype(jnp.int32)
    before = orders + row_ids[:, None] * GC
    labels = jax.vmap(lambda sub_key: jax.random.permutation(sub_key, LANES))(jax.random.split(key_labels, GR)).astype(jnp.int32)
    offsets = jax.vmap(lambda sub_key: jnp.repeat(jax.random.permutation(sub_key, LANES - 1) + 1, 2)[:MOVE_OUT])(jax.random.split(key_offsets, GR)).astype(jnp.int32)
    leaving = jax.vmap(lambda sub_key: jax.random.permutation(sub_key, TILE_DEV)[:MOVE_OUT])(jax.random.split(key_leave, GR * LANES)).astype(jnp.int32)
    flat_leave = leaving.reshape(GR, LANES * MOVE_OUT)
    positions = jnp.arange(LANES, dtype=jnp.int32)
    job_index = jnp.arange(MOVE_OUT, dtype=jnp.int32)[None, None, :]
    sender_pos = (positions[None, :, None] - offsets[:, None, :]) % LANES
    sender_lane = jnp.take_along_axis(labels, sender_pos.reshape(GR, LANES * MOVE_OUT), axis=1).reshape(GR, LANES, MOVE_OUT)
    receiver_lane = jnp.broadcast_to(labels[:, :, None], (GR, LANES, MOVE_OUT))
    into_slot = jnp.take_along_axis(flat_leave, (receiver_lane * MOVE_OUT + job_index).reshape(GR, LANES * MOVE_OUT), axis=1)
    from_slot = jnp.take_along_axis(flat_leave, (sender_lane * MOVE_OUT + job_index).reshape(GR, LANES * MOVE_OUT), axis=1)
    target = receiver_lane.reshape(GR, LANES * MOVE_OUT) * TILE_DEV + into_slot
    source = sender_lane.reshape(GR, LANES * MOVE_OUT) * TILE_DEV + from_slot
    moved_ids = jnp.take_along_axis(before, source, axis=1)
    after = jax.vmap(lambda row_data, spots, values: row_data.at[spots].set(values))(before, target, moved_ids)
    return (before.reshape(GR * GC).astype(jnp.int32), after.reshape(GR * GC).astype(jnp.int32))


def draw_placed_before(key, part):
    return tile_layouts(key)[0]


def draw_placed_after(key, part):
    return tile_layouts(key)[1]


def place_ends(values, key, least, top_value):
    shape = values.shape
    index_at = [jax.random.randint(jax.random.fold_in(key, axis), (), 0, shape[axis]) for axis in range(len(shape))]
    values = values.at[tuple(index_at)].set(least)
    longest = shape.index(max(shape))
    index_at[longest] = (index_at[longest] + 1) % shape[longest]
    return values.at[tuple(index_at)].set(top_value)


def block_levels(own_key, dims, pieces, low, largest):
    def one(axis_at, blocks):
        heights = jax.random.uniform(jax.random.fold_in(jax.random.fold_in(own_key, 6), axis_at), (blocks,), jnp.float32, low / len(pieces), largest / len(pieces))
        return jnp.repeat(jnp.exp(heights), dims[axis_at] // blocks).reshape((-1,) + (1,) * (len(dims) - axis_at - 1))

    level = one(*pieces[0])
    for cut in pieces[1:]:
        level = level * one(*cut)
    return level


def bell_draw(own_key, shape, deviation, most, cuts=(), held_as=jnp.bfloat16):
    result = deviation * jax.random.normal(own_key, shape, jnp.float32)
    if cuts:
        result = result * block_levels(own_key, shape, cuts, -0.22, 0.18)
    return jnp.clip(result, -most, most).astype(held_as)


def setup_inputs(seed: int = 0, part: int = 0) -> dict:
    keys = jax.random.split(jax.random.key(seed), 9)
    part_keys = jax.random.split(jax.random.fold_in(keys[8], part), 9)
    water_depth = jnp.clip(jnp.exp(math.log(3.0) - 3.4011974 * jax.random.uniform(part_keys[0], (TILES, TS, TS), jnp.float32) ** block_levels(part_keys[0], (TILES, TS, TS), ((0, 16),), -0.2, 0.2)), 0.1, 3.0)
    flow_east = bell_draw(part_keys[1], (TILES, TS, TS), 0.5, 3.0, ((0, 16),), jnp.float32)
    flow_south = bell_draw(part_keys[2], (TILES, TS, TS), 0.5, 3.0, ((0, 16),), jnp.float32)
    bed_level = bell_draw(part_keys[3], (TILES, TS, TS), 0.3, 2.0, ((0, 16),), jnp.float32)
    manning_n = jnp.clip(jnp.exp(math.log(0.15) - 1.609438 * jax.random.uniform(part_keys[4], (TILES, TS, TS), jnp.float32) ** block_levels(part_keys[4], (TILES, TS, TS), ((0, 16),), -0.2, 0.2)), 0.03, 0.15)
    placed_before = draw_placed_before(jax.random.fold_in(jax.random.fold_in(keys[8], part), 71), part)
    placed_after = draw_placed_after(jax.random.fold_in(jax.random.fold_in(keys[8], part), 71), part)
    wet_tiles = place_ends((jax.random.randint(part_keys[7], (TILES,), 0, 4) < 3).astype(jnp.int32), jax.random.fold_in(part_keys[7], 1), 0, 1)
    return dict(water_depth=water_depth, flow_east=flow_east, flow_south=flow_south, bed_level=bed_level, manning_n=manning_n, placed_before=placed_before, placed_after=placed_after, wet_tiles=wet_tiles)


GRAV = 9.81
STEP_TIME = 0.5
SPACING = 5.0
RATE = 0.1
DEPTH_FLOOR = 0.3


def face_flow(discharge, surface, surface_next, ground, ground_next, manning):
    wetted = jnp.maximum(surface, surface_next) - jnp.maximum(ground, ground_next)
    pressure = GRAV * STEP_TIME * jnp.maximum(wetted, 0.0) * (surface_next - surface) / SPACING
    resistance = 1.0 + GRAV * STEP_TIME * manning * manning * jnp.abs(discharge) / jnp.power(jnp.maximum(wetted, DEPTH_FLOOR), 7.0 / 3.0)
    return (discharge - pressure) / resistance


def inverse(ordering):
    entries = ordering.shape[0]
    return jnp.zeros((entries,), jnp.int32).at[ordering].set(jnp.arange(entries, dtype=jnp.int32))


def assemble(tile_data, where_before):
    ordered = tile_data[where_before]
    return ordered.reshape(GR, GC, TS, TS).transpose(0, 2, 1, 3).reshape(GR * TS, GC * TS)


def disperse(grid, placed_after):
    tile_data = grid.reshape(GR, TS, GC, TS).transpose(0, 2, 1, 3).reshape(GR * GC, TS, TS)
    return tile_data[placed_after]


def reference(water_depth, flow_east, flow_south, bed_level, manning_n, placed_before, placed_after, wet_tiles):
    where_before = inverse(placed_before)
    depth_now = assemble(water_depth, where_before)
    flow_x = assemble(flow_east, where_before)
    flow_y = assemble(flow_south, where_before)
    ground = assemble(bed_level, where_before)
    manning = assemble(manning_n, where_before)
    wet_cells = jnp.repeat(jnp.repeat((wet_tiles == 1).reshape(GR, GC), TS, axis=0), TS, axis=1)
    open_east = jnp.concatenate([wet_cells[:, :-1] & wet_cells[:, 1:], jnp.zeros((GR * TS, 1), jnp.bool_)], axis=1)
    open_south = jnp.concatenate([wet_cells[:-1, :] & wet_cells[1:, :], jnp.zeros((1, GC * TS), jnp.bool_)], axis=0)
    for step_index in range(STEPS):
        surface = depth_now + ground
        surface_east = jnp.concatenate([surface[:, 1:], surface[:, -1:]], axis=1)
        ground_east = jnp.concatenate([ground[:, 1:], ground[:, -1:]], axis=1)
        surface_south = jnp.concatenate([surface[1:, :], surface[-1:, :]], axis=0)
        ground_south = jnp.concatenate([ground[1:, :], ground[-1:, :]], axis=0)
        updated_x = face_flow(flow_x, surface, surface_east, ground, ground_east, manning)
        updated_y = face_flow(flow_y, surface, surface_south, ground, ground_south, manning)
        flow_x = jnp.where(wet_cells, jnp.where(open_east, updated_x, 0.0), flow_x)
        flow_y = jnp.where(wet_cells, jnp.where(open_south, updated_y, 0.0), flow_y)
        inflow_x = jnp.concatenate([jnp.zeros_like(flow_x[:, :1]), jnp.where(open_east[:, :-1], flow_x[:, :-1], 0.0)], axis=1)
        inflow_y = jnp.concatenate([jnp.zeros_like(flow_y[:1, :]), jnp.where(open_south[:-1, :], flow_y[:-1, :], 0.0)], axis=0)
        depth_now = jnp.where(wet_cells, depth_now + RATE * (((inflow_x - flow_x) + inflow_y) - flow_y), depth_now)
    return (disperse(depth_now, placed_after), disperse(flow_x, placed_after), disperse(flow_y, placed_after))
```

```python
import functools
import jax
import jax.numpy as jnp
from jax import lax
from jax.experimental import pallas as pl
from jax.experimental.pallas import tpu as pltpu
from jax.sharding import PartitionSpec as P

STEPS = 6
HALO = 6
MOVE = 4
PER_PEER = 2
GRAV = 9.81
STEP_TIME = 0.5
SPACING = 5.0
RATE = 0.1
DEPTH_FLOOR = 0.3
CLOSED = 1e30
SUBL = 8
LANE = 128
SEG = 12
HALF = 64
REC = 32
MESH_ID = pl.DeviceIdType.MESH
VMEM_LIMIT = 40 * 1024 * 1024

DIRS = ((0, -1), (0, 1), (-1, 0), (-1, -1), (-1, 1), (1, 0), (1, -1), (1, 1))


def table_kernel(tiles, lanes, rows, me_ref, pb_ref, pa_ref, wet_ref, tbl_ref, invb, inva, cnt):
    total = lanes * rows * tiles
    row_tiles = lanes * tiles
    my_row = me_ref[0]
    my_lane = me_ref[1]
    my_dev = my_row * lanes + my_lane

    def fill(s, _):
        invb[pb_ref[s]] = s
        inva[pa_ref[s]] = s
        return 0

    lax.fori_loop(0, total, fill, 0)
    for o in range(lanes):
        cnt[o] = 0

    def place(t, ranks):
        leave_rank, stay_rank = ranks
        tile = pb_ref[my_dev * tiles + t]
        dest = inva[tile] // tiles
        leaving = dest != my_dev
        pos = jnp.where(leaving, leave_rank, stay_rank)
        base = pos * REC
        tbl_ref[base] = t
        tbl_ref[base + 1] = wet_ref[tile]
        trow = tile // row_tiles
        tcol = tile % row_tiles
        for d, (dr, dc) in enumerate(DIRS):
            r, c = trow + dr, tcol + dc
            exists = (r >= 0) & (r < rows) & (c >= 0) & (c < row_tiles)
            other = jnp.where(exists, r * row_tiles + c, 0)
            where = invb[other] % row_tiles
            tbl_ref[base + 2 + d] = jnp.where(exists, wet_ref[other], 0)
            tbl_ref[base + 10 + 2 * d] = where // tiles
            tbl_ref[base + 11 + 2 * d] = where % tiles
        off = lax.rem(dest % lanes - my_lane + lanes, lanes)
        k = cnt[off]
        cnt[off] = k + 1
        tbl_ref[base + 26] = off
        tbl_ref[base + 27] = k
        lv = leaving.astype(jnp.int32)
        return leave_rank + lv, stay_rank + 1 - lv

    lax.fori_loop(0, tiles, place, (jnp.int32(0), jnp.int32(MOVE)))

    def final(s, _):
        src = invb[pa_ref[my_dev * tiles + s]]
        src_dev = src // tiles
        off = lax.rem(my_lane - src_dev % lanes + lanes, lanes)

        def rank(j, n):
            same = (inva[pb_ref[src_dev * tiles + j]] // tiles == my_dev) & (j < src % tiles)
            return n + same.astype(jnp.int32)

        n = lax.fori_loop(0, tiles, rank, jnp.int32(0))
        tbl_ref[tiles * REC + 2 * s] = off
        tbl_ref[tiles * REC + 2 * s + 1] = n
        return 0

    lax.fori_loop(0, tiles, final, 0)


def halo_kernel(tiles, h, x, y, z, m, gc, gu, gd, top, bot, ssem, rsem, vs, vr):
    cols = lax.axis_size("col")
    rows = lax.axis_size("row")
    b = lax.axis_index("basin")
    r = lax.axis_index("row")
    c = lax.axis_index("col")
    s = lax.axis_index("sub")
    other = 1 - s
    me = c * 2 + s
    sib = c * 2 + other
    fields = (h, x, y, z, m)

    barrier = pltpu.get_barrier_semaphore()
    pl.semaphore_signal(barrier, inc=1, device_id=(b, r, c, other), device_id_type=MESH_ID)
    for d in range(1, cols):
        pl.semaphore_signal(
            barrier, inc=1, device_id=(b, r, lax.rem(c + d, cols), s), device_id_type=MESH_ID
        )

    @pl.when(r > 0)
    def _():
        pl.semaphore_signal(barrier, inc=1, device_id=(b, r - 1, c, s), device_id_type=MESH_ID)

    @pl.when(r < rows - 1)
    def _():
        pl.semaphore_signal(barrier, inc=1, device_id=(b, r + 1, c, s), device_id_type=MESH_ID)

    for f in range(5):
        top[:, f] = fields[f][:, 0:SUBL, :]
        bot[:, f] = fields[f][:, LANE - SUBL : LANE, :]

    beside = jnp.where(r > 0, 1, 0) + jnp.where(r < rows - 1, 1, 0)
    pl.semaphore_wait(barrier, cols + beside)

    def up_copy():
        return pltpu.make_async_remote_copy(
            top, gd.at[me], vs.at[0], vr.at[0], device_id=(b, r - 1, c, s), device_id_type=MESH_ID
        )

    def down_copy():
        return pltpu.make_async_remote_copy(
            bot, gu.at[me], vs.at[1], vr.at[1], device_id=(b, r + 1, c, s), device_id_type=MESH_ID
        )

    @pl.when(r > 0)
    def _():
        up_copy().start()

    @pl.when(r < rows - 1)
    def _():
        down_copy().start()

    lane = lax.broadcasted_iota(jnp.int32, (SUBL, LANE), 1)

    def pack(i, _):
        blk = i // (LANE // SUBL)
        row = pl.multiple_of((i % (LANE // SUBL)) * SUBL, SUBL)
        acc = jnp.zeros((SUBL, LANE), jnp.float32)
        for u in range(2):
            for f in range(5):
                base = u * HALF + f * SEG
                v = fields[f][2 * blk + u, pl.ds(row, SUBL), :]
                v = pltpu.roll(v, (base - (LANE - HALO)) % LANE, 1)
                acc = jnp.where((lane >= base) & (lane < base + SEG), v, acc)
        gc[me, blk, pl.ds(row, SUBL), :] = acc
        return 0

    lax.fori_loop(0, (tiles // 2) * (LANE // SUBL), pack, 0)

    bufs = (gc, gu, gd)

    def across(kind, d):
        return pltpu.make_async_remote_copy(
            bufs[kind].at[me],
            bufs[kind].at[me],
            ssem.at[kind, d],
            rsem.at[kind, me],
            device_id=(b, r, lax.rem(c + d, cols), s),
            device_id_type=MESH_ID,
        )

    def sideways(kind, src_col, d):
        slot = src_col * 2 + s
        return pltpu.make_async_remote_copy(
            bufs[kind].at[slot],
            bufs[kind].at[slot],
            ssem.at[kind, cols + d],
            rsem.at[kind, slot],
            device_id=(b, r, c, other),
            device_id_type=MESH_ID,
        )

    def arrived(kind, slot):
        pltpu.make_async_remote_copy(
            bufs[kind].at[slot],
            bufs[kind].at[slot],
            ssem.at[kind, 0],
            rsem.at[kind, slot],
            device_id=(b, r, c, other),
            device_id_type=MESH_ID,
        ).wait_recv()

    def spread(kind):
        for d in range(1, cols):
            across(kind, d).start()
        sideways(kind, c, 0).start()

    def relay(kind):
        for d in range(1, cols):
            src = lax.rem(c + d, cols)
            arrived(kind, src * 2 + s)
            sideways(kind, src, d).start()

    def close(kind):
        for d in range(cols):
            src = lax.rem(c + d, cols)
            arrived(kind, src * 2 + other)
        for d in range(1, cols):
            across(kind, d).wait_send()
        for d in range(cols):
            sideways(kind, lax.rem(c + d, cols), d).wait_send()

    spread(0)

    @pl.when(r < rows - 1)
    def _():
        up_copy().wait_recv()
        spread(2)

    @pl.when(r > 0)
    def _():
        down_copy().wait_recv()
        spread(1)

    relay(0)

    @pl.when(r < rows - 1)
    def _():
        relay(2)

    @pl.when(r > 0)
    def _():
        relay(1)

    close(0)

    @pl.when(r < rows - 1)
    def _():
        close(2)
        down_copy().wait_send()

    @pl.when(r > 0)
    def _():
        close(1)
        up_copy().wait_send()


def steps_kernel(first, count, peers, tbl, h, x, y, z, m, gc, gu, gd, *rest):
    outs = rest[: max(peers, 1)]
    ph, px, py, pz, pm, mx, my, pw = rest[max(peers, 1) :]
    fields = (h, x, y, z, m)
    packs = (ph, px, py, pz, pm)
    width = ph.shape[1]
    nblk = width // LANE
    pitch = LANE + 2 * HALO
    nrow = LANE // SUBL
    chunks = nrow + 2
    lane = lax.broadcasted_iota(jnp.int32, (SUBL, LANE), 1)

    def put(acc, v, a, d, length):
        shift = (d - a) % LANE
        if shift:
            v = pltpu.roll(v, shift, 1)
        for k in range(d // LANE, (d + length - 1) // LANE + 1):
            lo = max(d - k * LANE, 0)
            hi = min(d + length - k * LANE, LANE)
            acc[k] = jnp.where((lane >= lo) & (lane < hi), v, acc[k])

    def rec(q, i):
        return tbl[(first + q) * REC + i]

    def fresh():
        return [jnp.zeros((SUBL, LANE), jnp.float32) for _ in range(nblk)]

    def save(ref, row, acc):
        ref[pl.ds(row, SUBL), :] = jnp.concatenate(acc, axis=1)

    def fill(i, _):
        row = pl.multiple_of(i * SUBL, SUBL)
        west, east = [], []
        for q in range(count):
            side = []
            for d in range(2):
                ln, sl = rec(q, 10 + 2 * d), rec(q, 11 + 2 * d)
                v = gc[ln, sl // 2, pl.ds(row, SUBL), :]
                v = jnp.where(sl % 2 == 1, pltpu.roll(v, HALF, 1), v)
                side.append(jnp.where(rec(q, 2 + d) == 1, v, 0.0))
            west.append(side[0])
            east.append(side[1])
        for f in range(5):
            acc = fresh()
            for q in range(count):
                at = q * pitch + HALO
                put(acc, fields[f][rec(q, 0), pl.ds(row, SUBL), :], 0, at, LANE)
                put(acc, west[q], f * SEG, at - HALO, HALO)
                put(acc, east[q], f * SEG + HALO, at + LANE, HALO)
            save(packs[f], row + SUBL, acc)
        return 0

    lax.fori_loop(0, nrow, fill, 0)
    for row, buf, d0 in ((0, gu, 2), (LANE + SUBL, gd, 5)):
        for f in range(5):
            acc = fresh()
            for q in range(count):
                at = q * pitch + HALO
                got = []
                for d in range(d0, d0 + 3):
                    v = buf[rec(q, 10 + 2 * d), rec(q, 11 + 2 * d), f]
                    got.append(jnp.where(rec(q, 2 + d) == 1, v, 0.0))
                put(acc, got[0], 0, at, LANE)
                put(acc, got[1], LANE - HALO, at - HALO, HALO)
                put(acc, got[2], 0, at + LANE, HALO)
            save(packs[f], row, acc)

    def wet_rows(cell, left, right):
        acc = fresh()
        for q in range(count):
            at = q * pitch + HALO
            for i, a, n in ((cell, at, LANE), (left, at - HALO, HALO), (right, at + LANE, HALO)):
                v = jnp.full((SUBL, LANE), (rec(q, i) == 1).astype(jnp.float32))
                put(acc, v, a, a, n)
        return jnp.concatenate(acc, axis=1)

    pw[0:SUBL, :] = wet_rows(4, 5, 6)
    pw[SUBL : 2 * SUBL, :] = wet_rows(1, 2, 3)
    pw[2 * SUBL : 3 * SUBL, :] = wet_rows(7, 8, 9)

    full = (SUBL, width)
    sub = lax.broadcasted_iota(jnp.int32, full, 0)
    last_row = sub == SUBL - 1
    first_row = sub == 0

    def ready(i, _):
        row = pl.multiple_of(i * SUBL, SUBL)
        nxt = pl.multiple_of(jnp.minimum(i + 1, chunks - 1) * SUBL, SUBL)
        kind = jnp.where(i == 0, 0, jnp.where(i == chunks - 1, 2, 1))
        kind2 = jnp.where(i + 1 >= chunks - 1, 2, 1)
        w = pw[pl.ds(pl.multiple_of(kind * SUBL, SUBL), SUBL), :]
        w2 = pw[pl.ds(pl.multiple_of(kind2 * SUBL, SUBL), SUBL), :]
        ww = pltpu.roll(w, width - 1, 1)
        ws = jnp.where(last_row, w2, w)
        zz = pz[pl.ds(row, SUBL), :]
        zn = pz[pl.ds(nxt, SUBL), :]
        ze = pltpu.roll(zz, width - 1, 1)
        zs = pltpu.roll(jnp.where(first_row, zn, zz), SUBL - 1, 0)
        ox = w * ww > 0.5
        oy = w * ws > 0.5
        mx[pl.ds(row, SUBL), :] = jnp.where(ox, jnp.maximum(zz, ze), CLOSED)
        my[pl.ds(row, SUBL), :] = jnp.where(oy, jnp.maximum(zz, zs), CLOSED)
        px[pl.ds(row, SUBL), :] = jnp.where(ox, px[pl.ds(row, SUBL), :], 0.0)
        py[pl.ds(row, SUBL), :] = jnp.where(oy, py[pl.ds(row, SUBL), :], 0.0)
        mm = pm[pl.ds(row, SUBL), :]
        pm[pl.ds(row, SUBL), :] = (GRAV * STEP_TIME) * mm * mm
        return 0

    lax.fori_loop(0, chunks, ready, 0)

    def face(q, e, e2, mz, mm):
        f = jnp.maximum(e, e2) - mz
        num = q - (GRAV * STEP_TIME / SPACING) * jnp.maximum(f, 0.0) * (e2 - e)
        g = jnp.exp((-7.0 / 3.0) * jnp.log(jnp.maximum(f, DEPTH_FLOOR)))
        return num / (1.0 + mm * jnp.abs(q) * g)

    def chunk(i, carry):
        e, qy_above = carry
        row = pl.multiple_of(i * SUBL, SUBL)
        nxt = pl.multiple_of(jnp.minimum(i + 1, chunks - 1) * SUBL, SUBL)
        en = ph[pl.ds(nxt, SUBL), :] + pz[pl.ds(nxt, SUBL), :]
        mm = pm[pl.ds(row, SUBL), :]
        ee = pltpu.roll(e, width - 1, 1)
        es = pltpu.roll(jnp.where(first_row, en, e), SUBL - 1, 0)
        qx = face(px[pl.ds(row, SUBL), :], e, ee, mx[pl.ds(row, SUBL), :], mm)
        px[pl.ds(row, SUBL), :] = qx
        qy = face(py[pl.ds(row, SUBL), :], e, es, my[pl.ds(row, SUBL), :], mm)
        py[pl.ds(row, SUBL), :] = qy
        xw = pltpu.roll(qx, 1, 1)
        yn = pltpu.roll(jnp.where(last_row, qy_above, qy), 1, 0)
        ph[pl.ds(row, SUBL), :] += RATE * (((xw - qx) + yn) - qy)
        return en, qy

    def step(n, _):
        e0 = ph[0:SUBL, :] + pz[0:SUBL, :]
        lax.fori_loop(0, chunks, chunk, (e0, jnp.zeros(full, jnp.float32)))
        return 0

    lax.fori_loop(0, STEPS, step, 0)

    def drain(i, _):
        row = pl.multiple_of(i * SUBL, SUBL)
        for f in range(3):
            v = packs[f][pl.ds(row + SUBL, SUBL), :]
            for q in range(count):
                at = q * pitch + HALO
                k, s = at // LANE, at % LANE
                lo = pltpu.roll(v[:, k * LANE : (k + 1) * LANE], LANE - s, 1)
                hi = pltpu.roll(v[:, (k + 1) * LANE : (k + 2) * LANE], LANE - s, 1)
                t = jnp.where(lane < LANE - s, lo, hi)
                if f > 0:
                    old = fields[f][rec(q, 0), pl.ds(row, SUBL), :]
                    t = jnp.where(rec(q, 1) == 1, t, old)
                if peers:
                    for o in range(peers):

                        @pl.when(rec(q, 26) == o + 1)
                        def _(o=o, q=q, t=t, f=f):
                            outs[o][f, rec(q, 27), pl.ds(row, SUBL), :] = t

                else:
                    outs[0][f, q, pl.ds(row, SUBL), :] = t
        return 0

    lax.fori_loop(0, nrow, drain, 0)


def final_kernel(tiles, peers, tbl, stay, *rest):
    got = rest[:peers]
    outs = rest[peers:]
    s = pl.program_id(0)
    off = tbl[tiles * REC + 2 * s]
    k = tbl[tiles * REC + 2 * s + 1]

    @pl.when(off == 0)
    def _():
        for f in range(3):
            outs[f][0] = stay[f, k]

    for o in range(peers):

        @pl.when(off == o + 1)
        def _(o=o):
            for f in range(3):
                outs[f][0] = got[o][f, k]


def shards(h, x, y, z, m, pb, pa, wet):
    tiles = h.shape[0]
    lanes = lax.axis_size(("col", "sub"))
    cols = lax.axis_size("col")
    rows = lax.axis_size("row")
    f32 = jnp.float32
    me = jnp.stack([lax.axis_index("row"), lax.axis_index(("col", "sub"))]).astype(jnp.int32)
    smem = pl.BlockSpec(memory_space=pltpu.SMEM)
    vmem = pl.BlockSpec(memory_space=pltpu.VMEM)
    total = pb.shape[0]
    words = tiles * REC + 2 * tiles
    peers = lanes - 1
    tbl = pl.pallas_call(
        functools.partial(table_kernel, tiles, lanes, rows),
        out_shape=jax.ShapeDtypeStruct((words,), jnp.int32),
        in_specs=[smem] * 4,
        out_specs=smem,
        scratch_shapes=[
            pltpu.SMEM((total,), jnp.int32),
            pltpu.SMEM((total,), jnp.int32),
            pltpu.SMEM((lanes,), jnp.int32),
        ],
        name="tables",
    )(me, pb, pa, wet)
    ring = jax.ShapeDtypeStruct((lanes, tiles, 5, SUBL, LANE), f32)
    gc, gu, gd = pl.pallas_call(
        functools.partial(halo_kernel, tiles),
        out_shape=(jax.ShapeDtypeStruct((lanes, tiles // 2, LANE, LANE), f32), ring, ring),
        in_specs=[vmem] * 5,
        out_specs=(vmem,) * 3,
        scratch_shapes=[
            pltpu.VMEM((tiles, 5, SUBL, LANE), f32),
            pltpu.VMEM((tiles, 5, SUBL, LANE), f32),
            pltpu.SemaphoreType.DMA((3, 2 * cols)),
            pltpu.SemaphoreType.DMA((3, lanes)),
            pltpu.SemaphoreType.DMA((2,)),
            pltpu.SemaphoreType.DMA((2,)),
        ],
        compiler_params=pltpu.CompilerParams(
            collective_id=0, has_side_effects=True, vmem_limit_bytes=VMEM_LIMIT
        ),
        name="halo",
    )(h, x, y, z, m)

    def run(first, count, npeers):
        width = -(-count * (LANE + 2 * HALO) // LANE) * LANE
        slots = PER_PEER if npeers else count
        shape = jax.ShapeDtypeStruct((3, slots, LANE, LANE), f32)
        nout = max(npeers, 1)
        big = pltpu.VMEM((LANE + 2 * SUBL, width), f32)
        return pl.pallas_call(
            functools.partial(steps_kernel, first, count, npeers),
            out_shape=(shape,) * nout,
            in_specs=[smem] + [vmem] * 8,
            out_specs=(vmem,) * nout,
            scratch_shapes=[big] * 7 + [pltpu.VMEM((3 * SUBL, width), f32)],
            compiler_params=pltpu.CompilerParams(vmem_limit_bytes=VMEM_LIMIT),
            cost_estimate=pl.CostEstimate(
                flops=count * LANE * LANE * STEPS * 400, bytes_accessed=8 << 20, transcendentals=0
            ),
            name="steps",
        )(tbl, h, x, y, z, m, gc, gu, gd)

    sent = run(0, MOVE, peers)
    got = [
        lax.ppermute(sent[o - 1], ("col", "sub"), [(i, (i + o) % lanes) for i in range(lanes)])
        for o in range(1, lanes)
    ]
    (stay,) = run(MOVE, tiles - MOVE, 0)
    slot = pl.BlockSpec((1, LANE, LANE), lambda s: (s, 0, 0))
    return pl.pallas_call(
        functools.partial(final_kernel, tiles, peers),
        grid=(tiles,),
        out_shape=(jax.ShapeDtypeStruct(h.shape, f32),) * 3,
        in_specs=[smem] + [vmem] * (1 + peers),
        out_specs=(slot,) * 3,
        compiler_params=pltpu.CompilerParams(vmem_limit_bytes=VMEM_LIMIT),
        name="final",
    )(tbl, stay, *got)


def solution(mesh):
    tile = P(("basin", "row", "col", "sub"), None, None)
    part = P("basin")
    return jax.shard_map(
        shards,
        mesh=mesh,
        in_specs=(tile,) * 5 + (part,) * 3,
        out_specs=(tile,) * 3,
        check_vma=False,
    )
```

```python
import functools
import math
import jax
import jax.numpy as jnp
from jax import lax
from jax.experimental import pallas as pl
from jax.experimental.pallas import tpu as pltpu
from jax.sharding import PartitionSpec as P

STEPS = 6
HALO = 6
MOVE = 4
PER_PEER = 2
GRAV = 9.81
STEP_TIME = 0.5
SPACING = 5.0
RATE = 0.1
DEPTH_FLOOR = 0.3
CLOSED = 1e30
POWER = -7.0 / 3.0 / math.log(2.0)
UNROLL = 6
FILL = 4
READY = 3
DRAIN = 4
SUBL = 8
LANE = 128
SEG = 12
HALF = 64
REC = 32
EDGE = 32
MESH_ID = pl.DeviceIdType.MESH
VMEM_LIMIT = 40 * 1024 * 1024

DIRS = ((0, -1), (0, 1), (-1, 0), (-1, -1), (-1, 1), (1, 0), (1, -1), (1, 1))


def split(v, n):
    if n & (n - 1) == 0:
        return v >> (n.bit_length() - 1), v & (n - 1)
    return lax.div(v, n), lax.rem(v, n)


def table_kernel(tiles, pb_ref, pa_ref, wet_ref, tbl_ref, invb, inva, cnt):
    lanes = lax.axis_size("col") * lax.axis_size("sub")
    rows = lax.axis_size("row")
    total = lanes * rows * tiles
    row_tiles = lanes * tiles
    my_row = lax.axis_index("row")
    my_lane = lax.axis_index("col") * lax.axis_size("sub") + lax.axis_index("sub")
    my_dev = my_row * lanes + my_lane

    def fill(s, _):
        invb[pb_ref[s]] = s
        inva[pa_ref[s]] = s
        return 0

    lax.fori_loop(0, total, fill, 0, unroll=16)
    for o in range(lanes):
        cnt[o] = 0

    def place(t, ranks):
        leave_rank, stay_rank = ranks
        tile = pb_ref[my_dev * tiles + t]
        dest = split(inva[tile], tiles)[0]
        leaving = dest != my_dev
        pos = jnp.where(leaving, leave_rank, stay_rank)
        base = pos * REC
        tbl_ref[base] = t
        tbl_ref[base + 1] = wet_ref[tile]
        trow, tcol = split(tile, row_tiles)
        for d, (dr, dc) in enumerate(DIRS):
            r, c = trow + dr, tcol + dc
            exists = (r >= 0) & (r < rows) & (c >= 0) & (c < row_tiles)
            other = jnp.where(exists, r * row_tiles + c, 0)
            ln, sl = split(split(invb[other], row_tiles)[1], tiles)
            tbl_ref[base + 2 + d] = jnp.where(exists, wet_ref[other], 0)
            tbl_ref[base + 10 + 2 * d] = ln
            tbl_ref[base + 11 + 2 * d] = sl
        off = split(dest, lanes)[1] - my_lane
        off = jnp.where(off < 0, off + lanes, off)
        k = cnt[off]
        cnt[off] = k + 1
        tbl_ref[base + 26] = off
        tbl_ref[base + 27] = k
        lv = leaving.astype(jnp.int32)
        return leave_rank + lv, stay_rank + 1 - lv

    lax.fori_loop(0, tiles, place, (jnp.int32(0), jnp.int32(MOVE)))

    def final(s, _):
        src = invb[pa_ref[my_dev * tiles + s]]
        src_dev, src_slot = split(src, tiles)
        off = my_lane - split(src_dev, lanes)[1]
        off = jnp.where(off < 0, off + lanes, off)
        n = jnp.int32(0)
        for j in range(tiles):
            same = (split(inva[pb_ref[src_dev * tiles + j]], tiles)[0] == my_dev) & (j < src_slot)
            n = n + same.astype(jnp.int32)
        tbl_ref[tiles * REC + 2 * s] = off
        tbl_ref[tiles * REC + 2 * s + 1] = n
        return 0

    lax.fori_loop(0, tiles, final, 0)


def halo_kernel(tiles, *refs):
    cols = lax.axis_size("col")
    rows = lax.axis_size("row")
    b = lax.axis_index("basin")
    r = lax.axis_index("row")
    c = lax.axis_index("col")
    s = lax.axis_index("sub")
    other = 1 - s
    me = c * 2 + s
    sib = c * 2 + other
    fields, (gc, gu, gd, top, bot), (ssem, rsem, vs, vr) = refs[:5], refs[5:10], refs[10:]

    barrier = pltpu.get_barrier_semaphore()
    pl.semaphore_signal(barrier, inc=1, device_id=(b, r, c, other), device_id_type=MESH_ID)
    for d in range(1, cols):
        pl.semaphore_signal(
            barrier, inc=1, device_id=(b, r, lax.rem(c + d, cols), s), device_id_type=MESH_ID
        )

    @pl.when(r > 0)
    def _():
        pl.semaphore_signal(barrier, inc=1, device_id=(b, r - 1, c, s), device_id_type=MESH_ID)

    @pl.when(r < rows - 1)
    def _():
        pl.semaphore_signal(barrier, inc=1, device_id=(b, r + 1, c, s), device_id_type=MESH_ID)

    for t in range(tiles):
        first = [fields[f][t, 0:HALO, :] for f in range(5)]
        last = [fields[f][t, LANE - HALO : LANE, :] for f in range(5)]
        pad = [jnp.zeros((EDGE - 5 * HALO, LANE), jnp.float32)]
        top[t] = jnp.concatenate(first + pad, axis=0)
        bot[t] = jnp.concatenate(last + pad, axis=0)

    beside = jnp.where(r > 0, 1, 0) + jnp.where(r < rows - 1, 1, 0)
    pl.semaphore_wait(barrier, cols + beside)

    def up_copy():
        return pltpu.make_async_remote_copy(
            top, gd.at[me], vs.at[0], vr.at[0], device_id=(b, r - 1, c, s), device_id_type=MESH_ID
        )

    def down_copy():
        return pltpu.make_async_remote_copy(
            bot, gu.at[me], vs.at[1], vr.at[1], device_id=(b, r + 1, c, s), device_id_type=MESH_ID
        )

    @pl.when(r > 0)
    def _():
        up_copy().start()

    @pl.when(r < rows - 1)
    def _():
        down_copy().start()

    lane = lax.broadcasted_iota(jnp.int32, (SUBL, LANE), 1)

    def pack(i, _):
        blk = i // (LANE // SUBL)
        row = pl.multiple_of((i % (LANE // SUBL)) * SUBL, SUBL)
        acc = jnp.zeros((SUBL, LANE), jnp.float32)
        for u in range(2):
            for f in range(5):
                base = u * HALF + f * SEG
                v = fields[f][2 * blk + u, pl.ds(row, SUBL), :]
                v = pltpu.roll(v, (base - (LANE - HALO)) % LANE, 1)
                acc = jnp.where((lane >= base) & (lane < base + SEG), v, acc)
        gc[me, blk, pl.ds(row, SUBL), :] = acc
        return 0

    lax.fori_loop(0, (tiles // 2) * (LANE // SUBL), pack, 0, unroll=4)

    bufs = (gc, gu, gd)

    def across(kind, d):
        return pltpu.make_async_remote_copy(
            bufs[kind].at[me],
            bufs[kind].at[me],
            ssem.at[kind, d],
            rsem.at[kind, me],
            device_id=(b, r, lax.rem(c + d, cols), s),
            device_id_type=MESH_ID,
        )

    def sideways(kind, src_col, d):
        slot = src_col * 2 + s
        return pltpu.make_async_remote_copy(
            bufs[kind].at[slot],
            bufs[kind].at[slot],
            ssem.at[kind, cols + d],
            rsem.at[kind, slot],
            device_id=(b, r, c, other),
            device_id_type=MESH_ID,
        )

    def arrived(kind, slot):
        pltpu.make_async_remote_copy(
            bufs[kind].at[slot],
            bufs[kind].at[slot],
            ssem.at[kind, 0],
            rsem.at[kind, slot],
            device_id=(b, r, c, other),
            device_id_type=MESH_ID,
        ).wait_recv()

    def spread(kind):
        for d in range(1, cols):
            across(kind, d).start()
        sideways(kind, c, 0).start()

    def relay(kind):
        for d in range(1, cols):
            src = lax.rem(c + d, cols)
            arrived(kind, src * 2 + s)
            sideways(kind, src, d).start()

    def close(kind):
        for d in range(cols):
            src = lax.rem(c + d, cols)
            arrived(kind, src * 2 + other)
        for d in range(1, cols):
            across(kind, d).wait_send()
        for d in range(cols):
            sideways(kind, lax.rem(c + d, cols), d).wait_send()

    spread(0)

    @pl.when(r < rows - 1)
    def _():
        up_copy().wait_recv()
        spread(2)

    @pl.when(r > 0)
    def _():
        down_copy().wait_recv()
        spread(1)

    relay(0)

    @pl.when(r < rows - 1)
    def _():
        relay(2)

    @pl.when(r > 0)
    def _():
        relay(1)

    close(0)

    @pl.when(r < rows - 1)
    def _():
        close(2)
        down_copy().wait_send()

    @pl.when(r > 0)
    def _():
        close(1)
        up_copy().wait_send()


def steps_kernel(first, count, peers, tbl, h, x, y, z, m, gc, gu, gd, *rest):
    outs = rest[: max(peers, 1)]
    ph, px, py, pz, pm, mx, my, pw, hold = rest[max(peers, 1) :]
    fields = (h, x, y, z, m)
    packs = (ph, px, py, pz, pm)
    width = ph.shape[1]
    nblk = width // LANE
    pitch = LANE + 2 * HALO
    nrow = LANE // SUBL
    chunks = nrow + 2
    lane = lax.broadcasted_iota(jnp.int32, (SUBL, LANE), 1)

    def put(acc, v, a, d, length):
        shift = (d - a) % LANE
        if shift:
            v = pltpu.roll(v, shift, 1)
        for k in range(d // LANE, (d + length - 1) // LANE + 1):
            lo = max(d - k * LANE, 0)
            hi = min(d + length - k * LANE, LANE)
            acc[k] = jnp.where((lane >= lo) & (lane < hi), v, acc[k])

    def rec(q, i):
        return tbl[(first + q) * REC + i]

    def fresh():
        return [jnp.zeros((SUBL, LANE), jnp.float32) for _ in range(nblk)]

    def save(ref, row, acc):
        ref[pl.ds(row, SUBL), :] = jnp.concatenate(acc, axis=1)

    def fill(i, _):
        row = pl.multiple_of(i * SUBL, SUBL)
        west, east = [], []
        for q in range(count):
            side = []
            for d in range(2):
                ln, sl = rec(q, 10 + 2 * d), rec(q, 11 + 2 * d)
                v = gc[ln, sl // 2, pl.ds(row, SUBL), :]
                v = jnp.where(sl % 2 == 1, pltpu.roll(v, HALF, 1), v)
                side.append(jnp.where(rec(q, 2 + d) == 1, v, 0.0))
            west.append(side[0])
            east.append(side[1])
        for f in range(5):
            acc = fresh()
            for q in range(count):
                at = q * pitch + HALO
                put(acc, fields[f][rec(q, 0), pl.ds(row, SUBL), :], 0, at, LANE)
                put(acc, west[q], f * SEG, at - HALO, HALO)
                put(acc, east[q], f * SEG + HALO, at + LANE, HALO)
            save(packs[f], row + SUBL, acc)
        return 0

    lax.fori_loop(0, nrow, fill, 0, unroll=FILL)
    for row, buf, d0, lead in ((0, gu, 2, SUBL - HALO), (LANE + SUBL, gd, 5, 0)):
        for f in range(5):
            acc = fresh()
            for q in range(count):
                at = q * pitch + HALO
                got = []
                for d in range(d0, d0 + 3):
                    v = buf[rec(q, 10 + 2 * d), rec(q, 11 + 2 * d)]
                    v = pltpu.roll(v, (lead - f * HALO) % EDGE, 0)[0:SUBL]
                    got.append(jnp.where(rec(q, 2 + d) == 1, v, 0.0))
                put(acc, got[0], 0, at, LANE)
                put(acc, got[1], LANE - HALO, at - HALO, HALO)
                put(acc, got[2], 0, at + LANE, HALO)
            save(packs[f], row, acc)

    def wet_rows(cell, left, right):
        acc = fresh()
        for q in range(count):
            at = q * pitch + HALO
            for i, a, n in ((cell, at, LANE), (left, at - HALO, HALO), (right, at + LANE, HALO)):
                v = jnp.full((SUBL, LANE), (rec(q, i) == 1).astype(jnp.float32))
                put(acc, v, a, a, n)
        return jnp.concatenate(acc, axis=1)

    pw[0:SUBL, :] = wet_rows(4, 5, 6)
    pw[SUBL : 2 * SUBL, :] = wet_rows(1, 2, 3)
    pw[2 * SUBL : 3 * SUBL, :] = wet_rows(7, 8, 9)

    full = (SUBL, width)
    sub = lax.broadcasted_iota(jnp.int32, full, 0)
    last_row = sub == SUBL - 1
    first_row = sub == 0

    def ready(i, _):
        row = pl.multiple_of(i * SUBL, SUBL)
        nxt = pl.multiple_of(jnp.minimum(i + 1, chunks - 1) * SUBL, SUBL)
        kind = jnp.where(i == 0, 0, jnp.where(i == chunks - 1, 2, 1))
        kind2 = jnp.where(i + 1 >= chunks - 1, 2, 1)
        w = pw[pl.ds(pl.multiple_of(kind * SUBL, SUBL), SUBL), :]
        w2 = pw[pl.ds(pl.multiple_of(kind2 * SUBL, SUBL), SUBL), :]
        ww = pltpu.roll(w, width - 1, 1)
        ws = jnp.where(last_row, w2, w)
        zz = pz[pl.ds(row, SUBL), :]
        zn = pz[pl.ds(nxt, SUBL), :]
        ze = pltpu.roll(zz, width - 1, 1)
        zs = pltpu.roll(jnp.where(first_row, zn, zz), SUBL - 1, 0)
        ox = w * ww > 0.5
        oy = w * ws > 0.5
        mx[pl.ds(row, SUBL), :] = jnp.where(ox, jnp.maximum(zz, ze), CLOSED)
        my[pl.ds(row, SUBL), :] = jnp.where(oy, jnp.maximum(zz, zs), CLOSED)
        px[pl.ds(row, SUBL), :] = jnp.where(ox, px[pl.ds(row, SUBL), :], 0.0)
        py[pl.ds(row, SUBL), :] = jnp.where(oy, py[pl.ds(row, SUBL), :], 0.0)
        mm = pm[pl.ds(row, SUBL), :]
        pm[pl.ds(row, SUBL), :] = (GRAV * STEP_TIME) * mm * mm
        return 0

    lax.fori_loop(0, chunks, ready, 0, unroll=READY)

    def face(q, e, e2, mz, mm):
        f = jnp.maximum(e, e2) - mz
        num = q - (GRAV * STEP_TIME / SPACING) * jnp.maximum(f, 0.0) * (e2 - e)
        g = jnp.exp2(POWER * jnp.log(jnp.maximum(f, DEPTH_FLOOR)))
        return num, 1.0 + mm * jnp.abs(q) * g

    def chunk(i, carry):
        e, qy_above = carry
        row = pl.multiple_of(i * SUBL, SUBL)
        nxt = pl.multiple_of(jnp.minimum(i + 1, chunks - 1) * SUBL, SUBL)
        en = ph[pl.ds(nxt, SUBL), :] + pz[pl.ds(nxt, SUBL), :]
        mm = pm[pl.ds(row, SUBL), :]
        ee = pltpu.roll(e, width - 1, 1)
        es = pltpu.roll(jnp.where(first_row, en, e), SUBL - 1, 0)
        nx, rx = face(px[pl.ds(row, SUBL), :], e, ee, mx[pl.ds(row, SUBL), :], mm)
        ny, ry = face(py[pl.ds(row, SUBL), :], e, es, my[pl.ds(row, SUBL), :], mm)
        qx = nx / rx
        qy = ny / ry
        px[pl.ds(row, SUBL), :] = qx
        py[pl.ds(row, SUBL), :] = qy
        xw = pltpu.roll(qx, 1, 1)
        yn = pltpu.roll(jnp.where(last_row, qy_above, qy), 1, 0)
        ph[pl.ds(row, SUBL), :] += RATE * (((xw - qx) + yn) - qy)
        return en, qy

    def step(n, _):
        e0 = ph[0:SUBL, :] + pz[0:SUBL, :]
        lax.fori_loop(0, chunks, chunk, (e0, jnp.zeros(full, jnp.float32)), unroll=UNROLL)
        return 0

    lax.fori_loop(0, STEPS, step, 0)

    def drain(i, _):
        row = pl.multiple_of(i * SUBL, SUBL)
        for f in range(3):
            v = packs[f][pl.ds(row + SUBL, SUBL), :]
            for q in range(count):
                at = q * pitch + HALO
                k, s = at // LANE, at % LANE
                lo = pltpu.roll(v[:, k * LANE : (k + 1) * LANE], LANE - s, 1)
                hi = pltpu.roll(v[:, (k + 1) * LANE : (k + 2) * LANE], LANE - s, 1)
                t = jnp.where(lane < LANE - s, lo, hi)
                if f > 0:
                    old = fields[f][rec(q, 0), pl.ds(row, SUBL), :]
                    t = jnp.where(rec(q, 1) == 1, t, old)
                if peers:
                    slot = (rec(q, 26) - 1) * PER_PEER + rec(q, 27)
                    hold[slot, f, pl.ds(row, SUBL), :] = t
                else:
                    outs[0][f, q, pl.ds(row, SUBL), :] = t
        return 0

    lax.fori_loop(0, nrow, drain, 0, unroll=DRAIN)
    for o in range(peers):
        for k in range(PER_PEER):
            for f in range(3):
                outs[o][f, k] = hold[o * PER_PEER + k, f]


def final_kernel(tiles, peers, tbl, stay, *rest):
    got, outs, sem = rest[:peers], rest[peers : peers + 3], rest[-1]

    def send(ref, k, f, s):
        return pltpu.make_async_copy(ref.at[f, k], outs[f].at[s], sem.at[f, s])

    for s in range(tiles):
        off = tbl[tiles * REC + 2 * s]
        k = tbl[tiles * REC + 2 * s + 1]
        for o, ref in enumerate((stay,) + got):

            @pl.when(off == o)
            def _(ref=ref, k=k, s=s):
                for f in range(3):
                    send(ref, k, f, s).start()

    for s in range(tiles):
        for f in range(3):
            send(stay, 0, f, s).wait()


def shards(h, x, y, z, m, pb, pa, wet):
    tiles = h.shape[0]
    lanes = lax.axis_size(("col", "sub"))
    cols = lax.axis_size("col")
    f32 = jnp.float32
    smem = pl.BlockSpec(memory_space=pltpu.SMEM)
    vmem = pl.BlockSpec(memory_space=pltpu.VMEM)
    total = pb.shape[0]
    words = tiles * REC + 2 * tiles
    peers = lanes - 1
    tbl = pl.pallas_call(
        functools.partial(table_kernel, tiles),
        out_shape=jax.ShapeDtypeStruct((words,), jnp.int32),
        in_specs=[smem] * 3,
        out_specs=smem,
        scratch_shapes=[
            pltpu.SMEM((total,), jnp.int32),
            pltpu.SMEM((total,), jnp.int32),
            pltpu.SMEM((lanes,), jnp.int32),
        ],
        cost_estimate=pl.CostEstimate(
            flops=0, bytes_accessed=16 << 20, transcendentals=0
        ),
        name="tables",
    )(pb, pa, wet)
    ring = jax.ShapeDtypeStruct((lanes, tiles, EDGE, LANE), f32)
    gc, gu, gd = pl.pallas_call(
        functools.partial(halo_kernel, tiles),
        out_shape=(jax.ShapeDtypeStruct((lanes, tiles // 2, LANE, LANE), f32), ring, ring),
        in_specs=[vmem] * 5,
        out_specs=(vmem,) * 3,
        scratch_shapes=[pltpu.VMEM((tiles, EDGE, LANE), f32)] * 2
        + [
            pltpu.SemaphoreType.DMA((3, 2 * cols)),
            pltpu.SemaphoreType.DMA((3, lanes)),
            pltpu.SemaphoreType.DMA((2,)),
            pltpu.SemaphoreType.DMA((2,)),
        ],
        compiler_params=pltpu.CompilerParams(
            collective_id=0, has_side_effects=True, vmem_limit_bytes=VMEM_LIMIT
        ),
        name="halo",
    )(h, x, y, z, m)

    def run(first, count, npeers):
        width = -(-count * (LANE + 2 * HALO) // LANE) * LANE
        slots = PER_PEER if npeers else count
        shape = jax.ShapeDtypeStruct((3, slots, LANE, LANE), f32)
        nout = max(npeers, 1)
        big = pltpu.VMEM((LANE + 2 * SUBL, width), f32)
        return pl.pallas_call(
            functools.partial(steps_kernel, first, count, npeers),
            out_shape=(shape,) * nout,
            in_specs=[smem] + [vmem] * 8,
            out_specs=(vmem,) * nout,
            scratch_shapes=[big] * 7
            + [
                pltpu.VMEM((3 * SUBL, width), f32),
                pltpu.VMEM((max(npeers, 1) * PER_PEER, 3, LANE, LANE), f32),
            ],
            compiler_params=pltpu.CompilerParams(vmem_limit_bytes=VMEM_LIMIT),
            cost_estimate=pl.CostEstimate(
                flops=count * LANE * LANE * STEPS * 400, bytes_accessed=8 << 20, transcendentals=0
            ),
            name="steps",
        )(tbl, h, x, y, z, m, gc, gu, gd)

    sent = run(0, MOVE, peers)
    got = [
        lax.ppermute(sent[o - 1], ("col", "sub"), [(i, (i + o) % lanes) for i in range(lanes)])
        for o in range(1, lanes)
    ]
    (stay,) = run(MOVE, tiles - MOVE, 0)
    return pl.pallas_call(
        functools.partial(final_kernel, tiles, peers),
        out_shape=(jax.ShapeDtypeStruct(h.shape, f32),) * 3,
        in_specs=[smem] + [vmem] * (1 + peers),
        out_specs=(pl.BlockSpec(memory_space=pltpu.MemorySpace.HBM),) * 3,
        scratch_shapes=[pltpu.SemaphoreType.DMA((3, tiles))],
        compiler_params=pltpu.CompilerParams(vmem_limit_bytes=VMEM_LIMIT),
        name="final",
    )(tbl, stay, *got)


def solution(mesh):
    tile = P(("basin", "row", "col", "sub"), None, None)
    part = P("basin")
    return jax.shard_map(
        shards,
        mesh=mesh,
        in_specs=(tile,) * 5 + (part,) * 3,
        out_specs=(tile,) * 3,
        check_vma=False,
    )
```

```python
import functools
import math
import jax
import jax.numpy as jnp
from jax import lax
from jax.experimental import pallas as pl
from jax.experimental.pallas import tpu as pltpu
from jax.sharding import PartitionSpec as P

STEPS = 6
HALO = 6
MOVE = 4
PER_PEER = 2
GRAV = 9.81
STEP_TIME = 0.5
SPACING = 5.0
RATE = 0.1
DEPTH_FLOOR = 0.3
CLOSED = 1e30
POWER = -7.0 / 3.0 / math.log(2.0)
UNROLL = 18
FILL = 16
READY = 18
DRAIN = 16
SUBL = 8
LANE = 128
SEG = 12
HALF = 64
REC = 32
EDGE = 32
MESH_ID = pl.DeviceIdType.MESH
VMEM_LIMIT = 40 * 1024 * 1024

DIRS = ((0, -1), (0, 1), (-1, 0), (-1, -1), (-1, 1), (1, 0), (1, -1), (1, 1))


def split(v, n):
    if n & (n - 1) == 0:
        return v >> (n.bit_length() - 1), v & (n - 1)
    return lax.div(v, n), lax.rem(v, n)


def table_kernel(tiles, pb_ref, pa_ref, wet_ref, tbl_ref, invb, inva, cnt):
    lanes = lax.axis_size("col") * lax.axis_size("sub")
    rows = lax.axis_size("row")
    total = lanes * rows * tiles
    row_tiles = lanes * tiles
    my_row = lax.axis_index("row")
    my_lane = lax.axis_index("col") * lax.axis_size("sub") + lax.axis_index("sub")
    my_dev = my_row * lanes + my_lane

    def fill(s, _):
        invb[pb_ref[s]] = s
        inva[pa_ref[s]] = s
        return 0

    lax.fori_loop(0, total, fill, 0, unroll=16)
    for o in range(lanes):
        cnt[o] = 0

    def place(t, ranks):
        leave_rank, stay_rank = ranks
        tile = pb_ref[my_dev * tiles + t]
        dest = split(inva[tile], tiles)[0]
        leaving = dest != my_dev
        pos = jnp.where(leaving, leave_rank, stay_rank)
        base = pos * REC
        tbl_ref[base] = t
        tbl_ref[base + 1] = wet_ref[tile]
        trow, tcol = split(tile, row_tiles)
        for d, (dr, dc) in enumerate(DIRS):
            r, c = trow + dr, tcol + dc
            exists = (r >= 0) & (r < rows) & (c >= 0) & (c < row_tiles)
            other = jnp.where(exists, r * row_tiles + c, 0)
            ln, sl = split(split(invb[other], row_tiles)[1], tiles)
            tbl_ref[base + 2 + d] = jnp.where(exists, wet_ref[other], 0)
            tbl_ref[base + 10 + 2 * d] = ln
            tbl_ref[base + 11 + 2 * d] = sl
        off = split(dest, lanes)[1] - my_lane
        off = jnp.where(off < 0, off + lanes, off)
        k = cnt[off]
        cnt[off] = k + 1
        tbl_ref[base + 26] = off
        tbl_ref[base + 27] = k
        lv = leaving.astype(jnp.int32)
        return leave_rank + lv, stay_rank + 1 - lv

    lax.fori_loop(0, tiles, place, (jnp.int32(0), jnp.int32(MOVE)))

    def final(s, _):
        src = invb[pa_ref[my_dev * tiles + s]]
        src_dev, src_slot = split(src, tiles)
        off = my_lane - split(src_dev, lanes)[1]
        off = jnp.where(off < 0, off + lanes, off)
        n = jnp.int32(0)
        for j in range(tiles):
            same = (split(inva[pb_ref[src_dev * tiles + j]], tiles)[0] == my_dev) & (j < src_slot)
            n = n + same.astype(jnp.int32)
        tbl_ref[tiles * REC + 2 * s] = off
        tbl_ref[tiles * REC + 2 * s + 1] = n
        return 0

    lax.fori_loop(0, tiles, final, 0)


def halo_kernel(tiles, *refs):
    cols = lax.axis_size("col")
    rows = lax.axis_size("row")
    b = lax.axis_index("basin")
    r = lax.axis_index("row")
    c = lax.axis_index("col")
    s = lax.axis_index("sub")
    other = 1 - s
    me = c * 2 + s
    sib = c * 2 + other
    fields, (gc, gu, gd, top, bot), (ssem, rsem, vs, vr) = refs[:5], refs[5:10], refs[10:]

    barrier = pltpu.get_barrier_semaphore()
    pl.semaphore_signal(barrier, inc=1, device_id=(b, r, c, other), device_id_type=MESH_ID)
    for d in range(1, cols):
        pl.semaphore_signal(
            barrier, inc=1, device_id=(b, r, lax.rem(c + d, cols), s), device_id_type=MESH_ID
        )

    @pl.when(r > 0)
    def _():
        pl.semaphore_signal(barrier, inc=1, device_id=(b, r - 1, c, s), device_id_type=MESH_ID)

    @pl.when(r < rows - 1)
    def _():
        pl.semaphore_signal(barrier, inc=1, device_id=(b, r + 1, c, s), device_id_type=MESH_ID)

    for t in range(tiles):
        first = [fields[f][t, 0:HALO, :] for f in range(5)]
        last = [fields[f][t, LANE - HALO : LANE, :] for f in range(5)]
        pad = [jnp.zeros((EDGE - 5 * HALO, LANE), jnp.float32)]
        top[t] = jnp.concatenate(first + pad, axis=0)
        bot[t] = jnp.concatenate(last + pad, axis=0)

    beside = jnp.where(r > 0, 1, 0) + jnp.where(r < rows - 1, 1, 0)
    pl.semaphore_wait(barrier, cols + beside)

    def up_copy():
        return pltpu.make_async_remote_copy(
            top, gd.at[me], vs.at[0], vr.at[0], device_id=(b, r - 1, c, s), device_id_type=MESH_ID
        )

    def down_copy():
        return pltpu.make_async_remote_copy(
            bot, gu.at[me], vs.at[1], vr.at[1], device_id=(b, r + 1, c, s), device_id_type=MESH_ID
        )

    @pl.when(r > 0)
    def _():
        up_copy().start()

    @pl.when(r < rows - 1)
    def _():
        down_copy().start()

    lane = lax.broadcasted_iota(jnp.int32, (SUBL, LANE), 1)

    def pack(i, _):
        blk = i // (LANE // SUBL)
        row = pl.multiple_of((i % (LANE // SUBL)) * SUBL, SUBL)
        acc = jnp.zeros((SUBL, LANE), jnp.float32)
        for u in range(2):
            for f in range(5):
                base = u * HALF + f * SEG
                v = fields[f][2 * blk + u, pl.ds(row, SUBL), :]
                v = pltpu.roll(v, (base - (LANE - HALO)) % LANE, 1)
                acc = jnp.where((lane >= base) & (lane < base + SEG), v, acc)
        gc[me, blk, pl.ds(row, SUBL), :] = acc
        return 0

    lax.fori_loop(0, (tiles // 2) * (LANE // SUBL), pack, 0, unroll=4)

    bufs = (gc, gu, gd)

    def across(kind, d):
        return pltpu.make_async_remote_copy(
            bufs[kind].at[me],
            bufs[kind].at[me],
            ssem.at[kind, d],
            rsem.at[kind, me],
            device_id=(b, r, lax.rem(c + d, cols), s),
            device_id_type=MESH_ID,
        )

    def sideways(kind, src_col, d):
        slot = src_col * 2 + s
        return pltpu.make_async_remote_copy(
            bufs[kind].at[slot],
            bufs[kind].at[slot],
            ssem.at[kind, cols + d],
            rsem.at[kind, slot],
            device_id=(b, r, c, other),
            device_id_type=MESH_ID,
        )

    def arrived(kind, slot):
        pltpu.make_async_remote_copy(
            bufs[kind].at[slot],
            bufs[kind].at[slot],
            ssem.at[kind, 0],
            rsem.at[kind, slot],
            device_id=(b, r, c, other),
            device_id_type=MESH_ID,
        ).wait_recv()

    def spread(kind):
        for d in range(1, cols):
            across(kind, d).start()
        sideways(kind, c, 0).start()

    def relay(kind):
        for d in range(1, cols):
            src = lax.rem(c + d, cols)
            arrived(kind, src * 2 + s)
            sideways(kind, src, d).start()

    def close(kind):
        for d in range(cols):
            src = lax.rem(c + d, cols)
            arrived(kind, src * 2 + other)
        for d in range(1, cols):
            across(kind, d).wait_send()
        for d in range(cols):
            sideways(kind, lax.rem(c + d, cols), d).wait_send()

    spread(0)

    @pl.when(r < rows - 1)
    def _():
        up_copy().wait_recv()
        spread(2)

    @pl.when(r > 0)
    def _():
        down_copy().wait_recv()
        spread(1)

    relay(0)

    @pl.when(r < rows - 1)
    def _():
        relay(2)

    @pl.when(r > 0)
    def _():
        relay(1)

    close(0)

    @pl.when(r < rows - 1)
    def _():
        close(2)
        down_copy().wait_send()

    @pl.when(r > 0)
    def _():
        close(1)
        up_copy().wait_send()


def steps_kernel(first, count, peers, tbl, h, x, y, z, m, gc, gu, gd, *rest):
    outs = rest[: max(peers, 1)]
    ph, px, py, pz, pm, mx, my, pw, hold = rest[max(peers, 1) :]
    fields = (h, x, y, z, m)
    packs = (ph, px, py, pz, pm)
    width = ph.shape[1]
    nblk = width // LANE
    pitch = LANE + 2 * HALO
    nrow = LANE // SUBL
    chunks = nrow + 2
    lane = lax.broadcasted_iota(jnp.int32, (SUBL, LANE), 1)

    def put(acc, v, a, d, length):
        shift = (d - a) % LANE
        if shift:
            v = pltpu.roll(v, shift, 1)
        for k in range(d // LANE, (d + length - 1) // LANE + 1):
            lo = max(d - k * LANE, 0)
            hi = min(d + length - k * LANE, LANE)
            acc[k] = jnp.where((lane >= lo) & (lane < hi), v, acc[k])

    def rec(q, i):
        return tbl[(first + q) * REC + i]

    def fresh():
        return [jnp.zeros((SUBL, LANE), jnp.float32) for _ in range(nblk)]

    def save(ref, row, acc):
        ref[pl.ds(row, SUBL), :] = jnp.concatenate(acc, axis=1)

    def fill(i, _):
        row = pl.multiple_of(i * SUBL, SUBL)
        west, east = [], []
        for q in range(count):
            side = []
            for d in range(2):
                ln, sl = rec(q, 10 + 2 * d), rec(q, 11 + 2 * d)
                v = gc[ln, sl // 2, pl.ds(row, SUBL), :]
                v = jnp.where(sl % 2 == 1, pltpu.roll(v, HALF, 1), v)
                side.append(jnp.where(rec(q, 2 + d) == 1, v, 0.0))
            west.append(side[0])
            east.append(side[1])
        for f in range(5):
            acc = fresh()
            for q in range(count):
                at = q * pitch + HALO
                put(acc, fields[f][rec(q, 0), pl.ds(row, SUBL), :], 0, at, LANE)
                put(acc, west[q], f * SEG, at - HALO, HALO)
                put(acc, east[q], f * SEG + HALO, at + LANE, HALO)
            save(packs[f], row + SUBL, acc)
        return 0

    lax.fori_loop(0, nrow, fill, 0, unroll=FILL)
    for row, buf, d0, lead in ((0, gu, 2, SUBL - HALO), (LANE + SUBL, gd, 5, 0)):
        for f in range(5):
            acc = fresh()
            for q in range(count):
                at = q * pitch + HALO
                got = []
                for d in range(d0, d0 + 3):
                    v = buf[rec(q, 10 + 2 * d), rec(q, 11 + 2 * d)]
                    v = pltpu.roll(v, (lead - f * HALO) % EDGE, 0)[0:SUBL]
                    got.append(jnp.where(rec(q, 2 + d) == 1, v, 0.0))
                put(acc, got[0], 0, at, LANE)
                put(acc, got[1], LANE - HALO, at - HALO, HALO)
                put(acc, got[2], 0, at + LANE, HALO)
            save(packs[f], row, acc)

    def wet_rows(cell, left, right):
        acc = fresh()
        for q in range(count):
            at = q * pitch + HALO
            for i, a, n in ((cell, at, LANE), (left, at - HALO, HALO), (right, at + LANE, HALO)):
                v = jnp.full((SUBL, LANE), (rec(q, i) == 1).astype(jnp.float32))
                put(acc, v, a, a, n)
        return jnp.concatenate(acc, axis=1)

    pw[0:SUBL, :] = wet_rows(4, 5, 6)
    pw[SUBL : 2 * SUBL, :] = wet_rows(1, 2, 3)
    pw[2 * SUBL : 3 * SUBL, :] = wet_rows(7, 8, 9)

    full = (SUBL, width)
    sub = lax.broadcasted_iota(jnp.int32, full, 0)
    last_row = sub == SUBL - 1
    first_row = sub == 0

    def ready(i, _):
        row = pl.multiple_of(i * SUBL, SUBL)
        nxt = pl.multiple_of(jnp.minimum(i + 1, chunks - 1) * SUBL, SUBL)
        kind = jnp.where(i == 0, 0, jnp.where(i == chunks - 1, 2, 1))
        kind2 = jnp.where(i + 1 >= chunks - 1, 2, 1)
        w = pw[pl.ds(pl.multiple_of(kind * SUBL, SUBL), SUBL), :]
        w2 = pw[pl.ds(pl.multiple_of(kind2 * SUBL, SUBL), SUBL), :]
        ww = pltpu.roll(w, width - 1, 1)
        ws = jnp.where(last_row, w2, w)
        zz = pz[pl.ds(row, SUBL), :]
        zn = pz[pl.ds(nxt, SUBL), :]
        ze = pltpu.roll(zz, width - 1, 1)
        zs = pltpu.roll(jnp.where(first_row, zn, zz), SUBL - 1, 0)
        ox = w * ww > 0.5
        oy = w * ws > 0.5
        mx[pl.ds(row, SUBL), :] = jnp.where(ox, jnp.maximum(zz, ze), CLOSED)
        my[pl.ds(row, SUBL), :] = jnp.where(oy, jnp.maximum(zz, zs), CLOSED)
        px[pl.ds(row, SUBL), :] = jnp.where(ox, px[pl.ds(row, SUBL), :], 0.0)
        py[pl.ds(row, SUBL), :] = jnp.where(oy, py[pl.ds(row, SUBL), :], 0.0)
        mm = pm[pl.ds(row, SUBL), :]
        pm[pl.ds(row, SUBL), :] = (GRAV * STEP_TIME) * mm * mm
        return 0

    lax.fori_loop(0, chunks, ready, 0, unroll=READY)

    def face(q, e, e2, mz, mm):
        f = jnp.maximum(e, e2) - mz
        num = q - (GRAV * STEP_TIME / SPACING) * jnp.maximum(f, 0.0) * (e2 - e)
        g = jnp.exp2(POWER * jnp.log(jnp.maximum(f, DEPTH_FLOOR)))
        return num, 1.0 + mm * jnp.abs(q) * g

    def chunk(i, carry):
        e, qy_above = carry
        row = pl.multiple_of(i * SUBL, SUBL)
        nxt = pl.multiple_of(jnp.minimum(i + 1, chunks - 1) * SUBL, SUBL)
        en = ph[pl.ds(nxt, SUBL), :] + pz[pl.ds(nxt, SUBL), :]
        mm = pm[pl.ds(row, SUBL), :]
        ee = pltpu.roll(e, width - 1, 1)
        es = pltpu.roll(jnp.where(first_row, en, e), SUBL - 1, 0)
        nx, rx = face(px[pl.ds(row, SUBL), :], e, ee, mx[pl.ds(row, SUBL), :], mm)
        ny, ry = face(py[pl.ds(row, SUBL), :], e, es, my[pl.ds(row, SUBL), :], mm)
        qx = nx / rx
        qy = ny / ry
        px[pl.ds(row, SUBL), :] = qx
        py[pl.ds(row, SUBL), :] = qy
        xw = pltpu.roll(qx, 1, 1)
        yn = pltpu.roll(jnp.where(last_row, qy_above, qy), 1, 0)
        ph[pl.ds(row, SUBL), :] += RATE * (((xw - qx) + yn) - qy)
        return en, qy

    def step(n, _):
        e0 = ph[0:SUBL, :] + pz[0:SUBL, :]
        lax.fori_loop(0, chunks, chunk, (e0, jnp.zeros(full, jnp.float32)), unroll=UNROLL)
        return 0

    lax.fori_loop(0, STEPS, step, 0)

    def drain(i, _):
        row = pl.multiple_of(i * SUBL, SUBL)
        for f in range(3):
            v = packs[f][pl.ds(row + SUBL, SUBL), :]
            for q in range(count):
                at = q * pitch + HALO
                k, s = at // LANE, at % LANE
                lo = pltpu.roll(v[:, k * LANE : (k + 1) * LANE], LANE - s, 1)
                hi = pltpu.roll(v[:, (k + 1) * LANE : (k + 2) * LANE], LANE - s, 1)
                t = jnp.where(lane < LANE - s, lo, hi)
                if f > 0:
                    old = fields[f][rec(q, 0), pl.ds(row, SUBL), :]
                    t = jnp.where(rec(q, 1) == 1, t, old)
                if peers:
                    slot = (rec(q, 26) - 1) * PER_PEER + rec(q, 27)
                    hold[slot, f, pl.ds(row, SUBL), :] = t
                else:
                    outs[0][f, q, pl.ds(row, SUBL), :] = t
        return 0

    lax.fori_loop(0, nrow, drain, 0, unroll=DRAIN)
    for o in range(peers):
        for k in range(PER_PEER):
            for f in range(3):
                outs[o][f, k] = hold[o * PER_PEER + k, f]


def final_kernel(tiles, peers, tbl, stay, *rest):
    got, outs, sem = rest[:peers], rest[peers : peers + 3], rest[-1]

    def send(ref, k, f, s):
        return pltpu.make_async_copy(ref.at[f, k], outs[f].at[s], sem.at[f, s])

    for s in range(tiles):
        off = tbl[tiles * REC + 2 * s]
        k = tbl[tiles * REC + 2 * s + 1]
        for o, ref in enumerate((stay,) + got):

            @pl.when(off == o)
            def _(ref=ref, k=k, s=s):
                for f in range(3):
                    send(ref, k, f, s).start()

    for s in range(tiles):
        for f in range(3):
            send(stay, 0, f, s).wait()


def shards(h, x, y, z, m, pb, pa, wet):
    tiles = h.shape[0]
    lanes = lax.axis_size(("col", "sub"))
    cols = lax.axis_size("col")
    f32 = jnp.float32
    smem = pl.BlockSpec(memory_space=pltpu.SMEM)
    vmem = pl.BlockSpec(memory_space=pltpu.VMEM)
    total = pb.shape[0]
    words = tiles * REC + 2 * tiles
    peers = lanes - 1
    tbl = pl.pallas_call(
        functools.partial(table_kernel, tiles),
        out_shape=jax.ShapeDtypeStruct((words,), jnp.int32),
        in_specs=[smem] * 3,
        out_specs=smem,
        scratch_shapes=[
            pltpu.SMEM((total,), jnp.int32),
            pltpu.SMEM((total,), jnp.int32),
            pltpu.SMEM((lanes,), jnp.int32),
        ],
        cost_estimate=pl.CostEstimate(
            flops=4_000_000_000, bytes_accessed=16 << 20, transcendentals=0
        ),
        name="tables",
    )(pb, pa, wet)
    ring = jax.ShapeDtypeStruct((lanes, tiles, EDGE, LANE), f32)
    gc, gu, gd = pl.pallas_call(
        functools.partial(halo_kernel, tiles),
        out_shape=(jax.ShapeDtypeStruct((lanes, tiles // 2, LANE, LANE), f32), ring, ring),
        in_specs=[vmem] * 5,
        out_specs=(vmem,) * 3,
        scratch_shapes=[pltpu.VMEM((tiles, EDGE, LANE), f32)] * 2
        + [
            pltpu.SemaphoreType.DMA((3, 2 * cols)),
            pltpu.SemaphoreType.DMA((3, lanes)),
            pltpu.SemaphoreType.DMA((2,)),
            pltpu.SemaphoreType.DMA((2,)),
        ],
        compiler_params=pltpu.CompilerParams(
            collective_id=0, has_side_effects=True, vmem_limit_bytes=VMEM_LIMIT
        ),
        name="halo",
    )(h, x, y, z, m)

    def run(first, count, npeers):
        width = -(-count * (LANE + 2 * HALO) // LANE) * LANE
        slots = PER_PEER if npeers else count
        shape = jax.ShapeDtypeStruct((3, slots, LANE, LANE), f32)
        nout = max(npeers, 1)
        big = pltpu.VMEM((LANE + 2 * SUBL, width), f32)
        return pl.pallas_call(
            functools.partial(steps_kernel, first, count, npeers),
            out_shape=(shape,) * nout,
            in_specs=[smem] + [vmem] * 8,
            out_specs=(vmem,) * nout,
            scratch_shapes=[big] * 7
            + [
                pltpu.VMEM((3 * SUBL, width), f32),
                pltpu.VMEM((max(npeers, 1) * PER_PEER, 3, LANE, LANE), f32),
            ],
            compiler_params=pltpu.CompilerParams(vmem_limit_bytes=VMEM_LIMIT),
            cost_estimate=pl.CostEstimate(
                flops=count * LANE * LANE * STEPS * 400, bytes_accessed=8 << 20, transcendentals=0
            ),
            name="steps",
        )(tbl, h, x, y, z, m, gc, gu, gd)

    sent = run(0, MOVE, peers)
    got = [
        lax.ppermute(sent[o - 1], ("col", "sub"), [(i, (i + o) % lanes) for i in range(lanes)])
        for o in range(1, lanes)
    ]
    (stay,) = run(MOVE, tiles - MOVE, 0)
    return pl.pallas_call(
        functools.partial(final_kernel, tiles, peers),
        out_shape=(jax.ShapeDtypeStruct(h.shape, f32),) * 3,
        in_specs=[smem] + [vmem] * (1 + peers),
        out_specs=(pl.BlockSpec(memory_space=pltpu.MemorySpace.HBM),) * 3,
        scratch_shapes=[pltpu.SemaphoreType.DMA((3, tiles))],
        compiler_params=pltpu.CompilerParams(vmem_limit_bytes=VMEM_LIMIT),
        name="final",
    )(tbl, stay, *got)


def solution(mesh):
    tile = P(("basin", "row", "col", "sub"), None, None)
    part = P("basin")
    return jax.shard_map(
        shards,
        mesh=mesh,
        in_specs=(tile,) * 5 + (part,) * 3,
        out_specs=(tile,) * 3,
        check_vma=False,
    )
```

```python
import functools
import math
import jax
import jax.numpy as jnp
from jax import lax
from jax.experimental import pallas as pl
from jax.experimental.pallas import tpu as pltpu
from jax.sharding import PartitionSpec as P

STEPS = 6
HALO = 6
MOVE = 4
PER_PEER = 2
GRAV = 9.81
STEP_TIME = 0.5
SPACING = 5.0
RATE = 0.1
DEPTH_FLOOR = 0.3
CLOSED = 1e30
POWER = -7.0 / 3.0 / math.log(2.0)
UNROLL = 18
FILL = 16
READY = 18
DRAIN = 16
SUBL = 8
LANE = 128
SEG = 12
HALF = 64
REC = 32
EDGE = 32
MESH_ID = pl.DeviceIdType.MESH
VMEM_LIMIT = 40 * 1024 * 1024

DIRS = ((0, -1), (0, 1), (-1, 0), (-1, -1), (-1, 1), (1, 0), (1, -1), (1, 1))


def split(v, n):
    if n & (n - 1) == 0:
        return v >> (n.bit_length() - 1), v & (n - 1)
    return lax.div(v, n), lax.rem(v, n)


def table_kernel(tiles, pb_ref, pa_ref, wet_ref, tbl_ref, invb, inva, cnt):
    lanes = lax.axis_size("col") * lax.axis_size("sub")
    rows = lax.axis_size("row")
    total = lanes * rows * tiles
    row_tiles = lanes * tiles
    my_row = lax.axis_index("row")
    my_lane = lax.axis_index("col") * lax.axis_size("sub") + lax.axis_index("sub")
    my_dev = my_row * lanes + my_lane

    def fill(s, _):
        invb[pb_ref[s]] = s
        inva[pa_ref[s]] = s
        return 0

    lax.fori_loop(0, total, fill, 0, unroll=16)
    for o in range(lanes):
        cnt[o] = 0

    def place(t, ranks):
        leave_rank, stay_rank = ranks
        tile = pb_ref[my_dev * tiles + t]
        dest = split(inva[tile], tiles)[0]
        leaving = dest != my_dev
        pos = jnp.where(leaving, leave_rank, stay_rank)
        base = pos * REC
        tbl_ref[base] = t
        tbl_ref[base + 1] = wet_ref[tile]
        trow, tcol = split(tile, row_tiles)
        for d, (dr, dc) in enumerate(DIRS):
            r, c = trow + dr, tcol + dc
            exists = (r >= 0) & (r < rows) & (c >= 0) & (c < row_tiles)
            other = jnp.where(exists, r * row_tiles + c, 0)
            ln, sl = split(split(invb[other], row_tiles)[1], tiles)
            tbl_ref[base + 2 + d] = jnp.where(exists, wet_ref[other], 0)
            tbl_ref[base + 10 + 2 * d] = ln
            tbl_ref[base + 11 + 2 * d] = sl
        off = split(dest, lanes)[1] - my_lane
        off = jnp.where(off < 0, off + lanes, off)
        k = cnt[off]
        cnt[off] = k + 1
        tbl_ref[base + 26] = off
        tbl_ref[base + 27] = k
        lv = leaving.astype(jnp.int32)
        return leave_rank + lv, stay_rank + 1 - lv

    lax.fori_loop(0, tiles, place, (jnp.int32(0), jnp.int32(MOVE)))

    def final(s, _):
        src = invb[pa_ref[my_dev * tiles + s]]
        src_dev, src_slot = split(src, tiles)
        off = my_lane - split(src_dev, lanes)[1]
        off = jnp.where(off < 0, off + lanes, off)
        n = jnp.int32(0)
        for j in range(tiles):
            same = (split(inva[pb_ref[src_dev * tiles + j]], tiles)[0] == my_dev) & (j < src_slot)
            n = n + same.astype(jnp.int32)
        tbl_ref[tiles * REC + 2 * s] = off
        tbl_ref[tiles * REC + 2 * s + 1] = n
        return 0

    lax.fori_loop(0, tiles, final, 0)


def halo_kernel(tiles, *refs):
    cols = lax.axis_size("col")
    rows = lax.axis_size("row")
    b = lax.axis_index("basin")
    r = lax.axis_index("row")
    c = lax.axis_index("col")
    s = lax.axis_index("sub")
    other = 1 - s
    me = c * 2 + s
    sib = c * 2 + other
    fields, (gc, gu, gd, top, bot), (ssem, rsem, vs, vr) = refs[:5], refs[5:10], refs[10:]

    barrier = pltpu.get_barrier_semaphore()
    pl.semaphore_signal(barrier, inc=1, device_id=(b, r, c, other), device_id_type=MESH_ID)
    for d in range(1, cols):
        pl.semaphore_signal(
            barrier, inc=1, device_id=(b, r, lax.rem(c + d, cols), s), device_id_type=MESH_ID
        )

    @pl.when(r > 0)
    def _():
        pl.semaphore_signal(barrier, inc=1, device_id=(b, r - 1, c, s), device_id_type=MESH_ID)

    @pl.when(r < rows - 1)
    def _():
        pl.semaphore_signal(barrier, inc=1, device_id=(b, r + 1, c, s), device_id_type=MESH_ID)

    for t in range(tiles):
        first = [fields[f][t, 0:HALO, :] for f in range(5)]
        last = [fields[f][t, LANE - HALO : LANE, :] for f in range(5)]
        pad = [jnp.zeros((EDGE - 5 * HALO, LANE), jnp.float32)]
        top[t] = jnp.concatenate(first + pad, axis=0)
        bot[t] = jnp.concatenate(last + pad, axis=0)

    beside = jnp.where(r > 0, 1, 0) + jnp.where(r < rows - 1, 1, 0)
    pl.semaphore_wait(barrier, cols + beside)

    def up_copy():
        return pltpu.make_async_remote_copy(
            top, gd.at[me], vs.at[0], vr.at[0], device_id=(b, r - 1, c, s), device_id_type=MESH_ID
        )

    def down_copy():
        return pltpu.make_async_remote_copy(
            bot, gu.at[me], vs.at[1], vr.at[1], device_id=(b, r + 1, c, s), device_id_type=MESH_ID
        )

    @pl.when(r > 0)
    def _():
        up_copy().start()

    @pl.when(r < rows - 1)
    def _():
        down_copy().start()

    lane = lax.broadcasted_iota(jnp.int32, (SUBL, LANE), 1)

    def pack(blk):
        for row in range(0, LANE, SUBL):
            acc = jnp.zeros((SUBL, LANE), jnp.float32)
            for u in range(2):
                for f in range(5):
                    base = u * HALF + f * SEG
                    v = fields[f][2 * blk + u, row : row + SUBL, :]
                    v = pltpu.roll(v, (base - (LANE - HALO)) % LANE, 1)
                    acc = jnp.where((lane >= base) & (lane < base + SEG), v, acc)
            gc[me, blk, row : row + SUBL, :] = acc

    blocks = tiles // 2

    def part(kind, slot):
        return gc.at[slot, kind] if kind < blocks else (gu, gd)[kind - blocks].at[slot]

    def across(kind, d):
        return pltpu.make_async_remote_copy(
            part(kind, me),
            part(kind, me),
            ssem.at[kind, d],
            rsem.at[kind, me],
            device_id=(b, r, lax.rem(c + d, cols), s),
            device_id_type=MESH_ID,
        )

    def sideways(kind, src_col, d):
        slot = src_col * 2 + s
        return pltpu.make_async_remote_copy(
            part(kind, slot),
            part(kind, slot),
            ssem.at[kind, cols + d],
            rsem.at[kind, slot],
            device_id=(b, r, c, other),
            device_id_type=MESH_ID,
        )

    def arrived(kind, slot):
        pltpu.make_async_remote_copy(
            part(kind, slot),
            part(kind, slot),
            ssem.at[kind, 0],
            rsem.at[kind, slot],
            device_id=(b, r, c, other),
            device_id_type=MESH_ID,
        ).wait_recv()

    def spread(kind):
        for d in range(1, cols):
            across(kind, d).start()
        sideways(kind, c, 0).start()

    def relay(kind):
        for d in range(1, cols):
            src = lax.rem(c + d, cols)
            arrived(kind, src * 2 + s)
            sideways(kind, src, d).start()

    def close(kind):
        for d in range(cols):
            src = lax.rem(c + d, cols)
            arrived(kind, src * 2 + other)
        for d in range(1, cols):
            across(kind, d).wait_send()
        for d in range(cols):
            sideways(kind, lax.rem(c + d, cols), d).wait_send()

    for blk in range(blocks):
        pack(blk)
        spread(blk)

    @pl.when(r < rows - 1)
    def _():
        up_copy().wait_recv()
        spread(blocks + 1)

    @pl.when(r > 0)
    def _():
        down_copy().wait_recv()
        spread(blocks)

    for blk in range(blocks):
        relay(blk)

    @pl.when(r < rows - 1)
    def _():
        relay(blocks + 1)

    @pl.when(r > 0)
    def _():
        relay(blocks)

    for blk in range(blocks):
        close(blk)

    @pl.when(r < rows - 1)
    def _():
        close(blocks + 1)
        down_copy().wait_send()

    @pl.when(r > 0)
    def _():
        close(blocks)
        up_copy().wait_send()


def steps_kernel(first, count, peers, tbl, h, x, y, z, m, gc, gu, gd, *rest):
    outs = rest[: max(peers, 1)]
    ph, px, py, pz, pm, mx, my, pw, hold = rest[max(peers, 1) :]
    fields = (h, x, y, z, m)
    packs = (ph, px, py, pz, pm)
    width = ph.shape[1]
    nblk = width // LANE
    pitch = LANE + 2 * HALO
    nrow = LANE // SUBL
    chunks = nrow + 2
    lane = lax.broadcasted_iota(jnp.int32, (SUBL, LANE), 1)

    def put(acc, v, a, d, length):
        shift = (d - a) % LANE
        if shift:
            v = pltpu.roll(v, shift, 1)
        for k in range(d // LANE, (d + length - 1) // LANE + 1):
            lo = max(d - k * LANE, 0)
            hi = min(d + length - k * LANE, LANE)
            acc[k] = jnp.where((lane >= lo) & (lane < hi), v, acc[k])

    def rec(q, i):
        return tbl[(first + q) * REC + i]

    def fresh():
        return [jnp.zeros((SUBL, LANE), jnp.float32) for _ in range(nblk)]

    def save(ref, row, acc):
        ref[pl.ds(row, SUBL), :] = jnp.concatenate(acc, axis=1)

    def fill(i, _):
        row = pl.multiple_of(i * SUBL, SUBL)
        west, east = [], []
        for q in range(count):
            side = []
            for d in range(2):
                ln, sl = rec(q, 10 + 2 * d), rec(q, 11 + 2 * d)
                v = gc[ln, sl // 2, pl.ds(row, SUBL), :]
                v = jnp.where(sl % 2 == 1, pltpu.roll(v, HALF, 1), v)
                side.append(jnp.where(rec(q, 2 + d) == 1, v, 0.0))
            west.append(side[0])
            east.append(side[1])
        for f in range(5):
            acc = fresh()
            for q in range(count):
                at = q * pitch + HALO
                put(acc, fields[f][rec(q, 0), pl.ds(row, SUBL), :], 0, at, LANE)
                put(acc, west[q], f * SEG, at - HALO, HALO)
                put(acc, east[q], f * SEG + HALO, at + LANE, HALO)
            save(packs[f], row + SUBL, acc)
        return 0

    lax.fori_loop(0, nrow, fill, 0, unroll=FILL)
    for row, buf, d0, lead in ((0, gu, 2, SUBL - HALO), (LANE + SUBL, gd, 5, 0)):
        for f in range(5):
            acc = fresh()
            for q in range(count):
                at = q * pitch + HALO
                got = []
                for d in range(d0, d0 + 3):
                    v = buf[rec(q, 10 + 2 * d), rec(q, 11 + 2 * d)]
                    v = pltpu.roll(v, (lead - f * HALO) % EDGE, 0)[0:SUBL]
                    got.append(jnp.where(rec(q, 2 + d) == 1, v, 0.0))
                put(acc, got[0], 0, at, LANE)
                put(acc, got[1], LANE - HALO, at - HALO, HALO)
                put(acc, got[2], 0, at + LANE, HALO)
            save(packs[f], row, acc)

    def wet_rows(cell, left, right):
        acc = fresh()
        for q in range(count):
            at = q * pitch + HALO
            for i, a, n in ((cell, at, LANE), (left, at - HALO, HALO), (right, at + LANE, HALO)):
                v = jnp.full((SUBL, LANE), (rec(q, i) == 1).astype(jnp.float32))
                put(acc, v, a, a, n)
        return jnp.concatenate(acc, axis=1)

    pw[0:SUBL, :] = wet_rows(4, 5, 6)
    pw[SUBL : 2 * SUBL, :] = wet_rows(1, 2, 3)
    pw[2 * SUBL : 3 * SUBL, :] = wet_rows(7, 8, 9)

    full = (SUBL, width)
    sub = lax.broadcasted_iota(jnp.int32, full, 0)
    last_row = sub == SUBL - 1
    first_row = sub == 0

    def ready(i, _):
        row = pl.multiple_of(i * SUBL, SUBL)
        nxt = pl.multiple_of(jnp.minimum(i + 1, chunks - 1) * SUBL, SUBL)
        kind = jnp.where(i == 0, 0, jnp.where(i == chunks - 1, 2, 1))
        kind2 = jnp.where(i + 1 >= chunks - 1, 2, 1)
        w = pw[pl.ds(pl.multiple_of(kind * SUBL, SUBL), SUBL), :]
        w2 = pw[pl.ds(pl.multiple_of(kind2 * SUBL, SUBL), SUBL), :]
        ww = pltpu.roll(w, width - 1, 1)
        ws = jnp.where(last_row, w2, w)
        zz = pz[pl.ds(row, SUBL), :]
        zn = pz[pl.ds(nxt, SUBL), :]
        ze = pltpu.roll(zz, width - 1, 1)
        zs = pltpu.roll(jnp.where(first_row, zn, zz), SUBL - 1, 0)
        ox = w * ww > 0.5
        oy = w * ws > 0.5
        mx[pl.ds(row, SUBL), :] = jnp.where(ox, jnp.maximum(zz, ze), CLOSED)
        my[pl.ds(row, SUBL), :] = jnp.where(oy, jnp.maximum(zz, zs), CLOSED)
        px[pl.ds(row, SUBL), :] = jnp.where(ox, px[pl.ds(row, SUBL), :], 0.0)
        py[pl.ds(row, SUBL), :] = jnp.where(oy, py[pl.ds(row, SUBL), :], 0.0)
        mm = pm[pl.ds(row, SUBL), :]
        pm[pl.ds(row, SUBL), :] = (GRAV * STEP_TIME) * mm * mm
        return 0

    lax.fori_loop(0, chunks, ready, 0, unroll=READY)

    def face(q, e, e2, mz, mm):
        f = jnp.maximum(e, e2) - mz
        num = q - (GRAV * STEP_TIME / SPACING) * jnp.maximum(f, 0.0) * (e2 - e)
        g = jnp.exp2(POWER * jnp.log(jnp.maximum(f, DEPTH_FLOOR)))
        return num, 1.0 + mm * jnp.abs(q) * g

    def chunk(i, carry):
        e, qy_above = carry
        row = pl.multiple_of(i * SUBL, SUBL)
        nxt = pl.multiple_of(jnp.minimum(i + 1, chunks - 1) * SUBL, SUBL)
        en = ph[pl.ds(nxt, SUBL), :] + pz[pl.ds(nxt, SUBL), :]
        mm = pm[pl.ds(row, SUBL), :]
        ee = pltpu.roll(e, width - 1, 1)
        es = pltpu.roll(jnp.where(first_row, en, e), SUBL - 1, 0)
        nx, rx = face(px[pl.ds(row, SUBL), :], e, ee, mx[pl.ds(row, SUBL), :], mm)
        ny, ry = face(py[pl.ds(row, SUBL), :], e, es, my[pl.ds(row, SUBL), :], mm)
        qx = nx / rx
        qy = ny / ry
        px[pl.ds(row, SUBL), :] = qx
        py[pl.ds(row, SUBL), :] = qy
        xw = pltpu.roll(qx, 1, 1)
        yn = pltpu.roll(jnp.where(last_row, qy_above, qy), 1, 0)
        ph[pl.ds(row, SUBL), :] += RATE * (((xw - qx) + yn) - qy)
        return en, qy

    def step(n, _):
        e0 = ph[0:SUBL, :] + pz[0:SUBL, :]
        lax.fori_loop(0, chunks, chunk, (e0, jnp.zeros(full, jnp.float32)), unroll=UNROLL)
        return 0

    lax.fori_loop(0, STEPS, step, 0)

    def drain(i, _):
        row = pl.multiple_of(i * SUBL, SUBL)
        for f in range(3):
            v = packs[f][pl.ds(row + SUBL, SUBL), :]
            for q in range(count):
                at = q * pitch + HALO
                k, s = at // LANE, at % LANE
                lo = pltpu.roll(v[:, k * LANE : (k + 1) * LANE], LANE - s, 1)
                hi = pltpu.roll(v[:, (k + 1) * LANE : (k + 2) * LANE], LANE - s, 1)
                t = jnp.where(lane < LANE - s, lo, hi)
                if f > 0:
                    old = fields[f][rec(q, 0), pl.ds(row, SUBL), :]
                    t = jnp.where(rec(q, 1) == 1, t, old)
                if peers:
                    slot = (rec(q, 26) - 1) * PER_PEER + rec(q, 27)
                    hold[slot, f, pl.ds(row, SUBL), :] = t
                else:
                    outs[0][f, q, pl.ds(row, SUBL), :] = t
        return 0

    lax.fori_loop(0, nrow, drain, 0, unroll=DRAIN)
    for o in range(peers):
        for k in range(PER_PEER):
            for f in range(3):
                outs[o][f, k] = hold[o * PER_PEER + k, f]


def final_kernel(tiles, peers, tbl, stay, *rest):
    got, outs, sem = rest[:peers], rest[peers : peers + 3], rest[-1]

    def send(ref, k, f, s):
        return pltpu.make_async_copy(ref.at[f, k], outs[f].at[s], sem.at[f, s])

    for s in range(tiles):
        off = tbl[tiles * REC + 2 * s]
        k = tbl[tiles * REC + 2 * s + 1]
        for o, ref in enumerate((stay,) + got):

            @pl.when(off == o)
            def _(ref=ref, k=k, s=s):
                for f in range(3):
                    send(ref, k, f, s).start()

    for s in range(tiles):
        for f in range(3):
            send(stay, 0, f, s).wait()


def shards(h, x, y, z, m, pb, pa, wet):
    tiles = h.shape[0]
    lanes = lax.axis_size(("col", "sub"))
    cols = lax.axis_size("col")
    f32 = jnp.float32
    smem = pl.BlockSpec(memory_space=pltpu.SMEM)
    vmem = pl.BlockSpec(memory_space=pltpu.VMEM)
    total = pb.shape[0]
    words = tiles * REC + 2 * tiles
    peers = lanes - 1
    tbl = pl.pallas_call(
        functools.partial(table_kernel, tiles),
        out_shape=jax.ShapeDtypeStruct((words,), jnp.int32),
        in_specs=[smem] * 3,
        out_specs=smem,
        scratch_shapes=[
            pltpu.SMEM((total,), jnp.int32),
            pltpu.SMEM((total,), jnp.int32),
            pltpu.SMEM((lanes,), jnp.int32),
        ],
        cost_estimate=pl.CostEstimate(
            flops=4_000_000_000, bytes_accessed=16 << 20, transcendentals=0
        ),
        name="tables",
    )(pb, pa, wet)
    ring = jax.ShapeDtypeStruct((lanes, tiles, EDGE, LANE), f32)
    gc, gu, gd = pl.pallas_call(
        functools.partial(halo_kernel, tiles),
        out_shape=(jax.ShapeDtypeStruct((lanes, tiles // 2, LANE, LANE), f32), ring, ring),
        in_specs=[vmem] * 5,
        out_specs=(vmem,) * 3,
        scratch_shapes=[pltpu.VMEM((tiles, EDGE, LANE), f32)] * 2
        + [
            pltpu.SemaphoreType.DMA((tiles // 2 + 2, 2 * cols)),
            pltpu.SemaphoreType.DMA((tiles // 2 + 2, lanes)),
            pltpu.SemaphoreType.DMA((2,)),
            pltpu.SemaphoreType.DMA((2,)),
        ],
        compiler_params=pltpu.CompilerParams(
            collective_id=0, has_side_effects=True, vmem_limit_bytes=VMEM_LIMIT
        ),
        name="halo",
    )(h, x, y, z, m)

    def run(first, count, npeers):
        width = -(-count * (LANE + 2 * HALO) // LANE) * LANE
        slots = PER_PEER if npeers else count
        shape = jax.ShapeDtypeStruct((3, slots, LANE, LANE), f32)
        nout = max(npeers, 1)
        big = pltpu.VMEM((LANE + 2 * SUBL, width), f32)
        return pl.pallas_call(
            functools.partial(steps_kernel, first, count, npeers),
            out_shape=(shape,) * nout,
            in_specs=[smem] + [vmem] * 8,
            out_specs=(vmem,) * nout,
            scratch_shapes=[big] * 7
            + [
                pltpu.VMEM((3 * SUBL, width), f32),
                pltpu.VMEM((max(npeers, 1) * PER_PEER, 3, LANE, LANE), f32),
            ],
            compiler_params=pltpu.CompilerParams(vmem_limit_bytes=VMEM_LIMIT),
            cost_estimate=pl.CostEstimate(
                flops=count * LANE * LANE * STEPS * 400, bytes_accessed=8 << 20, transcendentals=0
            ),
            name="steps",
        )(tbl, h, x, y, z, m, gc, gu, gd)

    sent = run(0, MOVE, peers)
    got = [
        lax.ppermute(sent[o - 1], ("col", "sub"), [(i, (i + o) % lanes) for i in range(lanes)])
        for o in range(1, lanes)
    ]
    (stay,) = run(MOVE, tiles - MOVE, 0)
    return pl.pallas_call(
        functools.partial(final_kernel, tiles, peers),
        out_shape=(jax.ShapeDtypeStruct(h.shape, f32),) * 3,
        in_specs=[smem] + [vmem] * (1 + peers),
        out_specs=(pl.BlockSpec(memory_space=pltpu.MemorySpace.HBM),) * 3,
        scratch_shapes=[pltpu.SemaphoreType.DMA((3, tiles))],
        compiler_params=pltpu.CompilerParams(vmem_limit_bytes=VMEM_LIMIT),
        name="final",
    )(tbl, stay, *got)


def solution(mesh):
    tile = P(("basin", "row", "col", "sub"), None, None)
    part = P("basin")
    return jax.shard_map(
        shards,
        mesh=mesh,
        in_specs=(tile,) * 5 + (part,) * 3,
        out_specs=(tile,) * 3,
        check_vma=False,
    )
```
